32 devices in a mesh: blk: 16 (over z, y, x), col: 2 (over core).
Axes of the slice: x: 2, y: 2, z: 4, core: 2. Of those that a mesh axis runs over, the one named last changes fastest.
Arguments:
- trial: bfloat16 [32768, 128], P(('blk', 'col')), may hold values from -6 to 6
- omega: float32 [32768], P(('blk', 'col')), may hold values from 0.5 to 6
- table: bfloat16 [64, 128, 128], replicated, may hold values from -0.0625 to 0.0625
- block_type: int32 [256, 72], P(('blk', 'col')), may hold values from 0 to 63
- cycle_offset: int32 [256, 72], P(('blk', 'col')), may hold values from -4 to 4
- source_block: int32 [256, 72], P(('blk', 'col')), may hold values from 0 to 7
Outputs:
- sigma: bfloat16 [32768, 128], P(('blk', 'col'))
- projected: float32 [128, 128], replicated
- basis: float32 [32768, 128], P(('blk', 'col'))
The draws below stay inside these ranges and needn't reach their ends.
All inputs are finite; a program needn't handle non-finite values.
Results may differ from the reference program's by a relative error of at most 0.006.
Values may be sent and summed in bfloat16 or wider, within the bound.
A program may use at most 64 MiB of HBM per device.

```python
import jax
import jax.numpy as jnp
from jax import lax

K = 128
BLOCK = 128
RB_DEV = 8
NB = 72
NTYPE = 64
REACH = 4
RBLK = 256
PAIRS = 32768
N_BLK = 16
N_COL = 2


def draw_omega(key, part):
    uniform_part = jax.random.uniform(key, (PAIRS,), jnp.float32)
    ramp = 3.0 ** (jnp.arange(PAIRS, dtype=jnp.float32) / PAIRS)
    base = 0.5 * 4.0 ** uniform_part
    return base * ramp


def touch_ends(array, stream_key, least, top_value):
    extent = array.shape
    place = [jax.random.randint(jax.random.fold_in(stream_key, axis), (), 0, extent[axis]) for axis in range(len(extent))]
    array = array.at[tuple(place)].set(least)
    longest = extent.index(max(extent))
    place[longest] = (place[longest] + 1) % extent[longest]
    return array.at[tuple(place)].set(top_value)


def steps_of(own_key, shape, pieces, low, largest):
    gain = 1.0
    for axis_at, shards_of in pieces:
        draws = jax.random.uniform(jax.random.fold_in(jax.random.fold_in(own_key, 6), axis_at), (shards_of,), jnp.float32, low / len(pieces), largest / len(pieces))
        gain = gain * jnp.repeat(jnp.exp(draws), shape[axis_at] // shards_of).reshape((-1,) + (1,) * (len(shape) - 1 - axis_at))
    return gain


def normal_values(own_key, extent, scale, limit, pieces=(), kind=jnp.bfloat16):
    result = scale * jax.random.normal(own_key, extent, jnp.float32)
    if pieces:
        result = result * steps_of(own_key, extent, pieces, -0.22, 0.18)
    return jnp.clip(result, -limit, limit).astype(kind)


def setup_inputs(seed: int = 0) -> dict:
    key_of = jax.random.split(jax.random.key(seed), 7)
    return {
        "trial": normal_values(key_of[0], (PAIRS, K), 1.0, 6.0, ((0, 32),)),
        "omega": draw_omega(jax.random.fold_in(key_of[6], 71), 0),
        "table": normal_values(key_of[2], (NTYPE, BLOCK, BLOCK), (BLOCK * NB) ** -0.5, 0.0625),
        "block_type": touch_ends(jax.random.randint(key_of[3], (RBLK, NB), 0, NTYPE), jax.random.fold_in(key_of[3], 1), 0, NTYPE - 1).astype(jnp.int32),
        "cycle_offset": touch_ends(jax.random.randint(key_of[4], (RBLK, NB), 0 - REACH, REACH + 1), jax.random.fold_in(key_of[4], 1), 0 - REACH, REACH).astype(jnp.int32),
        "source_block": touch_ends(jax.random.randint(key_of[5], (RBLK, NB), 0, RB_DEV), jax.random.fold_in(key_of[5], 1), 0, RB_DEV - 1).astype(jnp.int32),
    }


def reference(trial, omega, table, block_type, cycle_offset, source_block):
    groups = N_BLK * N_COL
    trial_groups = trial.reshape(groups, RB_DEV, BLOCK, K)
    trial_five = trial.reshape(N_BLK, N_COL, RB_DEV, BLOCK, K)
    omega_groups = omega.reshape(groups, RB_DEV, BLOCK)
    type_groups = block_type.reshape(groups, RB_DEV, NB)
    cycle_groups = cycle_offset.reshape(groups, RB_DEV, NB)
    source_groups = source_block.reshape(groups, RB_DEV, NB)
    device_ids = jnp.arange(groups, dtype=jnp.int32)

    def one_group(operands):
        device_id, own_rows, energy, kinds, cycles, chosen = operands
        slab_id = device_id // N_COL
        column_id = device_id % N_COL
        far_slab = ((slab_id + cycles) % N_BLK).astype(jnp.int32)
        sources = trial_five[far_slab, column_id, chosen]
        coeffs = table[kinds]
        coupled = jnp.einsum('rjab,rjbk->rak', coeffs.astype(jnp.float32), sources.astype(jnp.float32))
        return (coupled + energy[:, :, None] * own_rows.astype(jnp.float32)).astype(jnp.bfloat16)
    sigma = lax.map(one_group, (device_ids, trial_groups, omega_groups, type_groups, cycle_groups, source_groups))
    sigma = sigma.reshape(PAIRS, K)
    highest = lax.Precision.HIGHEST
    sigma_full = sigma.astype(jnp.float32)
    trial_full = trial.astype(jnp.float32)
    projected = jnp.dot(trial_full.T, sigma_full, precision=highest) / PAIRS
    residual = sigma_full - jnp.dot(trial_full, projected, precision=highest)
    gram = jnp.dot(residual.T, residual, precision=highest) / PAIRS
    lower = jnp.linalg.cholesky(gram)
    inverse = jax.scipy.linalg.solve_triangular(lower, jnp.eye(K, dtype=jnp.float32), lower=True)
    basis = jnp.dot(residual, inverse.T, precision=highest)
    return (sigma, projected, basis)
```

```python
import functools

import jax
import jax.numpy as jnp
from jax import lax
from jax.experimental import pallas as pl
from jax.experimental.pallas import tpu as pltpu
from jax.sharding import PartitionSpec as P

REACH = 4
MESH = pl.DeviceIdType.MESH
HIGHEST = lax.Precision.HIGHEST
OFFSETS = [sign * step for step in range(REACH, 0, -1) for sign in (1, -1)]


def wrap(index, count):
    return lax.rem(index + count, count)


def dot_tn(left, right):
    return lax.dot_general(
        left, right, (((0,), (0,)), ((), ())), preferred_element_type=jnp.float32
    )


def couple_kernel(
    n_blk, n_col, near, kinds_ref, chosen_ref, trial_ref, omega_ref, table_hbm,
    sigma_ref, sums_ref,
    table_ref, slabs, part, gathered, ring, total,
    local_sems, g_send, g_recv, r_send, r_recv, z_send, z_recv, a_send, a_recv,
):
    blocks, pair_block, vec_count = trial_ref.shape
    per_row = kinds_ref.shape[1]
    rows = part.shape[0]
    me_b = lax.axis_index("blk")
    me_c = lax.axis_index("col")
    group = near * n_col
    far = n_blk // near
    piece = rows // group
    low = lax.rem(me_b, near)
    high = me_b // near
    mine = low * n_col + me_c

    def near_id(index):
        return (high * near + index // n_col, lax.rem(index, n_col))

    def far_id(index):
        return (index * near + low, me_c)

    load_table = pltpu.make_async_copy(table_hbm, table_ref, local_sems.at[0])
    load_table.start()
    keep_own = pltpu.make_async_copy(trial_ref, slabs.at[REACH], local_sems.at[1])
    keep_own.start()

    barrier = pltpu.get_barrier_semaphore()
    for offset in OFFSETS:
        pl.semaphore_signal(
            barrier, inc=1, device_id=(wrap(me_b - offset, n_blk), me_c), device_id_type=MESH
        )
    for step in range(1, group):
        pl.semaphore_signal(
            barrier, inc=1, device_id=near_id(wrap(mine + step, group)), device_id_type=MESH
        )
    for step in range(1, far):
        pl.semaphore_signal(
            barrier, inc=1, device_id=far_id(wrap(high + step, far)), device_id_type=MESH
        )
    pl.semaphore_wait(barrier, len(OFFSETS) + group - 1 + far - 1)

    sends = []
    for number, offset in enumerate(OFFSETS):
        copy = pltpu.make_async_remote_copy(
            src_ref=trial_ref,
            dst_ref=slabs.at[offset + REACH],
            send_sem=g_send.at[number],
            recv_sem=g_recv.at[number],
            device_id=(wrap(me_b - offset, n_blk), me_c),
            device_id_type=MESH,
        )
        copy.start()
        sends.append(copy)

    own = trial_ref[...].reshape(blocks * pair_block, vec_count)
    part[0:vec_count, :] = dot_tn(own, own)
    load_table.wait()
    keep_own.wait()
    for copy in sends:
        copy.wait()

    chunk = max(size for size in range(1, 9) if per_row % size == 0)
    row_id = lax.broadcasted_iota(jnp.int32, (pair_block, pair_block), 0)
    lane_id = lax.broadcasted_iota(jnp.int32, (pair_block, pair_block), 1)

    def one_block(r, carry):
        energy = jnp.broadcast_to(omega_ref[pl.ds(r, 1), :], (pair_block, pair_block))
        column = jnp.sum(jnp.where(row_id == lane_id, energy, 0.0), axis=1, keepdims=True)
        acc = column * trial_ref[r].astype(jnp.float32)
        for start in range(0, per_row, chunk):
            coeffs = []
            sources = []
            for j in range(start, start + chunk):
                coeffs.append(table_ref[kinds_ref[r, j]])
                tile = chosen_ref[r, j]
                sources.append(slabs[tile // blocks, lax.rem(tile, blocks)])
            acc = acc + jnp.dot(
                jnp.concatenate(coeffs, axis=1),
                jnp.concatenate(sources, axis=0),
                preferred_element_type=jnp.float32,
            )
        sigma_ref[pl.ds(pl.multiple_of(r * pair_block, pair_block), pair_block), :] = acc.astype(
            jnp.bfloat16
        )
        return carry

    lax.fori_loop(0, blocks, one_block, 0)

    sigma = sigma_ref[...]
    both = jnp.concatenate([own, sigma], axis=1)
    part[vec_count : 3 * vec_count, :] = dot_tn(both, sigma)

    copies = []
    for step in range(1, group):
        peer = wrap(mine + step, group)
        copy = pltpu.make_async_remote_copy(
            src_ref=part.at[pl.ds(pl.multiple_of(peer * piece, 8), piece)],
            dst_ref=gathered.at[step - 1],
            send_sem=r_send.at[step - 1],
            recv_sem=r_recv.at[step - 1],
            device_id=near_id(peer),
            device_id_type=MESH,
        )
        copy.start()
        copies.append(copy)
    piece_sum = part[pl.ds(pl.multiple_of(mine * piece, 8), piece), :]
    for step, copy in enumerate(copies):
        copy.wait()
        piece_sum = piece_sum + gathered[step]
    ring[high] = piece_sum

    copies = []
    for step in range(1, far):
        copy = pltpu.make_async_remote_copy(
            src_ref=ring.at[high],
            dst_ref=ring.at[high],
            send_sem=z_send.at[step - 1],
            recv_sem=z_recv.at[step - 1],
            device_id=far_id(wrap(high + step, far)),
            device_id_type=MESH,
        )
        copy.start()
        copies.append(copy)
    for copy in copies:
        copy.wait()
    piece_sum = ring[0]
    for index in range(1, far):
        piece_sum = piece_sum + ring[index]
    my_rows = pl.ds(pl.multiple_of(mine * piece, 8), piece)
    total[my_rows, :] = piece_sum

    copies = []
    for step in range(1, group):
        copy = pltpu.make_async_remote_copy(
            src_ref=total.at[my_rows],
            dst_ref=total.at[my_rows],
            send_sem=a_send.at[step - 1],
            recv_sem=a_recv.at[step - 1],
            device_id=near_id(wrap(mine + step, group)),
            device_id_type=MESH,
        )
        copy.start()
        copies.append(copy)
    for copy in copies:
        copy.wait()
    sums_ref[...] = total[...]


def split_three(value):
    high = value.astype(jnp.bfloat16)
    rest = value - high.astype(jnp.float32)
    middle = rest.astype(jnp.bfloat16)
    low = (rest - middle.astype(jnp.float32)).astype(jnp.bfloat16)
    return high, middle, low


def inverse_factor(gram):
    size = gram.shape[0]
    tiles = [gram[8 * t : 8 * t + 8, :] for t in range(size // 8)]
    lane = lax.broadcasted_iota(jnp.int32, (8, size), 1)
    sub = lax.broadcasted_iota(jnp.int32, (8, size), 0)
    for j in range(size):
        own, inner = j // 8, j % 8
        here = lane == j
        row = jnp.broadcast_to(tiles[own][inner : inner + 1, :], (8, size))
        pivot = jnp.broadcast_to(row[:, j : j + 1], (8, size))
        scaled = jnp.where(here, 1.0, row) * (1.0 / pivot)
        for t in range(own, size // 8):
            if t == own and inner == 7:
                continue
            column = jnp.broadcast_to(tiles[t][:, j : j + 1], (8, size))
            updated = jnp.where(here, 0.0, tiles[t]) - column * scaled
            tiles[t] = jnp.where(sub > inner, updated, tiles[t]) if t == own else updated
    inverse = []
    for t in range(size // 8):
        diagonal = lane == sub + 8 * t
        pivots = jnp.sum(jnp.where(diagonal, tiles[t], 0.0), axis=1, keepdims=True)
        unit = jnp.where(diagonal, 1.0, jnp.where(lane < sub + 8 * t, tiles[t], 0.0))
        inverse.append(unit / jnp.sqrt(pivots))
    return jnp.concatenate(inverse, axis=0)


def basis_kernel(total_rows, sums_ref, trial_ref, sigma_ref, projected_ref, basis_ref):
    size = sums_ref.shape[1]
    scale = 1.0 / total_rows
    overlap = sums_ref[0:size, :] * scale
    projected = sums_ref[size : 2 * size, :] * scale
    projected_ref[...] = projected
    square = sums_ref[2 * size : 3 * size, :] * scale
    row = lax.broadcasted_iota(jnp.int32, (size, size), 0)
    lane = lax.broadcasted_iota(jnp.int32, (size, size), 1)
    middle = jnp.where(row == lane, 2.0, 0.0) - overlap
    folded = jnp.dot(middle, projected, precision=HIGHEST, preferred_element_type=jnp.float32)
    gram = square - lax.dot_general(
        projected, folded, (((0,), (0,)), ((), ())),
        precision=HIGHEST, preferred_element_type=jnp.float32,
    )
    inverse = inverse_factor(gram)
    upper = inverse.T
    pulled = jnp.dot(projected, upper, precision=HIGHEST, preferred_element_type=jnp.float32)
    weights = jnp.concatenate([upper, 0.0 - pulled], axis=0)
    both = jnp.concatenate([sigma_ref[...], trial_ref[...]], axis=1)
    result = None
    for term in reversed(split_three(weights)):
        product = jnp.dot(both, term, preferred_element_type=jnp.float32)
        result = product if result is None else result + product
    basis_ref[...] = result


def on_device(n_blk, n_col, trial, omega, table, block_type, cycle_offset, source_block):
    row_count, vec_count = trial.shape
    pair_block = table.shape[1]
    blocks = row_count // pair_block
    near = max(size for size in (4, 2, 1) if n_blk % size == 0)
    group = near * n_col
    far = n_blk // near
    rows = 3 * vec_count
    piece = rows // group
    tile_index = (cycle_offset + REACH) * blocks + source_block
    vmem = pl.BlockSpec(memory_space=pltpu.VMEM)
    smem = pl.BlockSpec(memory_space=pltpu.SMEM)
    dma = pltpu.SemaphoreType.DMA
    sigma, sums = pl.pallas_call(
        functools.partial(couple_kernel, n_blk, n_col, near),
        out_shape=(
            jax.ShapeDtypeStruct((row_count, vec_count), jnp.bfloat16),
            jax.ShapeDtypeStruct((rows, vec_count), jnp.float32),
        ),
        in_specs=[smem, smem, vmem, vmem, pl.BlockSpec(memory_space=pl.ANY)],
        out_specs=(vmem, vmem),
        scratch_shapes=[
            pltpu.VMEM(table.shape, jnp.bfloat16),
            pltpu.VMEM((2 * REACH + 1, blocks, pair_block, vec_count), jnp.bfloat16),
            pltpu.VMEM((rows, vec_count), jnp.float32),
            pltpu.VMEM((group - 1, piece, vec_count), jnp.float32),
            pltpu.VMEM((far, piece, vec_count), jnp.float32),
            pltpu.VMEM((rows, vec_count), jnp.float32),
            dma((2,)),
            dma((2 * REACH,)),
            dma((2 * REACH,)),
            dma((group - 1,)),
            dma((group - 1,)),
            dma((far - 1,)),
            dma((far - 1,)),
            dma((group - 1,)),
            dma((group - 1,)),
        ],
        compiler_params=pltpu.CompilerParams(
            collective_id=0, has_side_effects=True, vmem_limit_bytes=32 << 20
        ),
        name="couple",
    )(
        block_type,
        tile_index,
        trial.reshape(blocks, pair_block, vec_count),
        omega.reshape(blocks, pair_block),
        table,
    )
    projected, basis = pl.pallas_call(
        functools.partial(basis_kernel, row_count * n_blk * n_col),
        out_shape=(
            jax.ShapeDtypeStruct((vec_count, vec_count), jnp.float32),
            jax.ShapeDtypeStruct((row_count, vec_count), jnp.float32),
        ),
        in_specs=[vmem] * 3,
        out_specs=(vmem, vmem),
        compiler_params=pltpu.CompilerParams(vmem_limit_bytes=32 << 20),
        name="basis",
    )(sums, trial, sigma)
    return (sigma, projected, basis)


def solution(mesh):
    placed = (
        P(("blk", "col"), None),
        P(("blk", "col")),
        P(),
        P(("blk", "col"), None),
        P(("blk", "col"), None),
        P(("blk", "col"), None),
    )
    return jax.shard_map(
        functools.partial(on_device, mesh.shape["blk"], mesh.shape["col"]),
        mesh=mesh,
        in_specs=placed,
        out_specs=(P(("blk", "col"), None), P(), P(("blk", "col"), None)),
        check_vma=False,
    )
```

```python
import functools

import jax
import jax.numpy as jnp
from jax import lax
from jax.experimental import pallas as pl
from jax.experimental.pallas import tpu as pltpu
from jax.sharding import PartitionSpec as P

REACH = 4
MESH = pl.DeviceIdType.MESH
HIGHEST = lax.Precision.HIGHEST
PARTS = 2


def wrap(index, count):
    return lax.rem(index + count, count)


def dot_tn(left, right):
    return lax.dot_general(
        left, right, (((0,), (0,)), ((), ())), preferred_element_type=jnp.float32
    )


def couple_kernel(
    n_blk, n_col, near,
    kinds_ref, cycle_ref, source_ref, trial_hbm, omega_hbm, table_hbm,
    sigma_ref, sums_ref,
    table_ref, slabs, omega_ref, part, gathered, ring, total,
    local_sems, g_send, g_recv, r_send, r_recv, z_send, z_recv, a_send, a_recv,
):
    blocks, pair_block, vec_count = trial_hbm.shape
    per_row = kinds_ref.shape[1]
    rows = part.shape[0]
    me_b = lax.axis_index("blk")
    me_c = lax.axis_index("col")
    group = near * n_col
    far = n_blk // near
    piece = rows // group
    low = lax.rem(me_b, near)
    high = me_b // near
    mine = low * n_col + me_c

    def near_id(index):
        return (high * near + index // n_col, lax.rem(index, n_col))

    def far_id(index):
        return (index * near + low, me_c)

    keep_own = pltpu.make_async_copy(trial_hbm, slabs.at[REACH], local_sems.at[0])
    keep_own.start()
    load_omega = pltpu.make_async_copy(omega_hbm, omega_ref, local_sems.at[1])
    load_omega.start()
    load_table = pltpu.make_async_copy(table_hbm, table_ref, local_sems.at[2])
    load_table.start()

    barrier = pltpu.get_barrier_semaphore()
    for step in range(1, far):
        pl.semaphore_signal(
            barrier, inc=1, device_id=far_id(wrap(high + step, far)), device_id_type=MESH
        )
    for step in range(1, group):
        pl.semaphore_signal(
            barrier, inc=1, device_id=near_id(wrap(mine + step, group)), device_id_type=MESH
        )
    pl.semaphore_wait(barrier, group - 1 + far - 1)

    x = lax.rem(low, 2)
    y = low // 2
    up = wrap(me_b + REACH, n_blk)
    down = wrap(me_b - REACH, n_blk)
    side_x = me_b + 1 - 2 * x
    side_y = me_b + 2 - 4 * y
    span = blocks // PARTS

    def message(number, h, source, slot, target):
        rows_of = pl.ds(h * span, span)
        return pltpu.make_async_remote_copy(
            src_ref=trial_hbm.at[rows_of] if source is None else slabs.at[source, rows_of],
            dst_ref=slabs.at[slot, rows_of],
            send_sem=g_send.at[number, h],
            recv_sem=g_recv.at[number, h],
            device_id=(target, me_c),
            device_id_type=MESH,
        )

    halves = range(PARTS)
    to_up = [message(0, h, None, 0, up) for h in halves]
    to_down = [message(1, h, None, 2 * REACH, down) for h in halves]
    own_x = [message(2, h, None, 3 + 2 * x, side_x) for h in halves]
    own_y = [message(3, h, None, 2 + 4 * y, side_y) for h in halves]
    pass_y = [message(4, h, 5 - 2 * x, 3 - 2 * x + 4 * y, side_y) for h in halves]
    far_x = [message(5, h, 8 - 8 * x, 7 - 6 * x, side_x) for h in halves]
    far_y = [message(6, h, 8 - 8 * y, 6 - 4 * y, side_y) for h in halves]
    pass_x = [message(7, h, 2 + 4 * y, 1 + 4 * y + 2 * x, side_x) for h in halves]

    def far_arrival(bit, h):
        return pltpu.make_async_remote_copy(
            src_ref=trial_hbm.at[pl.ds(h * span, span)],
            dst_ref=slabs.at[8 - 8 * bit, pl.ds(h * span, span)],
            send_sem=g_send.at[1 - bit, h],
            recv_sem=g_recv.at[1 - bit, h],
            device_id=(up, me_c),
            device_id_type=MESH,
        )

    for h in halves:
        to_up[h].start()
        to_down[h].start()
        own_x[h].start()
        own_y[h].start()

    keep_own.wait()
    own = slabs[REACH].reshape(blocks * pair_block, vec_count)
    part[0:vec_count, :] = dot_tn(own, own)

    for h in halves:
        own_x[h].wait_recv()
        pass_y[h].start()
    for h in halves:
        far_arrival(x, h).wait_recv()
        far_x[h].start()

        @pl.when(x == y)
        def _():
            far_y[h].start()

    for h in halves:
        far_arrival(1 - x, h).wait_recv()

        @pl.when(x != y)
        def _():
            far_y[h].start()

    for h in halves:
        far_y[h].wait_recv()
        pass_x[h].start()
    load_omega.wait()
    load_table.wait()
    for h in halves:
        own_y[h].wait_recv()
        pass_y[h].wait_recv()
        far_x[h].wait_recv()
        pass_x[h].wait_recv()
    for sent in (to_up, to_down, own_x, own_y, pass_y, far_x, far_y, pass_x):
        for h in halves:
            sent[h].wait_send()

    chunk = max(size for size in range(1, 9) if per_row % size == 0)
    row_id = lax.broadcasted_iota(jnp.int32, (pair_block, pair_block), 0)
    lane_id = lax.broadcasted_iota(jnp.int32, (pair_block, pair_block), 1)

    def one_block(r, carry):
        energy = jnp.broadcast_to(omega_ref[pl.ds(r, 1), :], (pair_block, pair_block))
        column = jnp.sum(jnp.where(row_id == lane_id, energy, 0.0), axis=1, keepdims=True)
        acc = column * slabs[REACH, r].astype(jnp.float32)
        for start in range(0, per_row, chunk):
            coeffs = []
            sources = []
            for j in range(start, start + chunk):
                coeffs.append(table_ref[kinds_ref[r, j]])
                sources.append(slabs[cycle_ref[r, j] + REACH, source_ref[r, j]])
            acc = acc + jnp.dot(
                jnp.concatenate(coeffs, axis=1),
                jnp.concatenate(sources, axis=0),
                preferred_element_type=jnp.float32,
            )
        sigma_ref[pl.ds(pl.multiple_of(r * pair_block, pair_block), pair_block), :] = acc.astype(
            jnp.bfloat16
        )
        return carry

    lax.fori_loop(0, blocks, one_block, 0)

    sigma = sigma_ref[...]
    both = jnp.concatenate([own, sigma], axis=1)
    part[vec_count : 3 * vec_count, :] = dot_tn(both, sigma)

    copies = []
    for step in range(1, group):
        peer = wrap(mine + step, group)
        copy = pltpu.make_async_remote_copy(
            src_ref=part.at[pl.ds(pl.multiple_of(peer * piece, 8), piece)],
            dst_ref=gathered.at[step - 1],
            send_sem=r_send.at[step - 1],
            recv_sem=r_recv.at[step - 1],
            device_id=near_id(peer),
            device_id_type=MESH,
        )
        copy.start()
        copies.append(copy)
    piece_sum = part[pl.ds(pl.multiple_of(mine * piece, 8), piece), :]
    for step, copy in enumerate(copies):
        copy.wait()
        piece_sum = piece_sum + gathered[step]
    ring[high] = piece_sum

    copies = []
    for step in range(1, far):
        copy = pltpu.make_async_remote_copy(
            src_ref=ring.at[high],
            dst_ref=ring.at[high],
            send_sem=z_send.at[step - 1],
            recv_sem=z_recv.at[step - 1],
            device_id=far_id(wrap(high + step, far)),
            device_id_type=MESH,
        )
        copy.start()
        copies.append(copy)
    for copy in copies:
        copy.wait()
    piece_sum = ring[0]
    for index in range(1, far):
        piece_sum = piece_sum + ring[index]
    my_rows = pl.ds(pl.multiple_of(mine * piece, 8), piece)
    total[my_rows, :] = piece_sum

    copies = []
    for step in range(1, group):
        copy = pltpu.make_async_remote_copy(
            src_ref=total.at[my_rows],
            dst_ref=total.at[my_rows],
            send_sem=a_send.at[step - 1],
            recv_sem=a_recv.at[step - 1],
            device_id=near_id(wrap(mine + step, group)),
            device_id_type=MESH,
        )
        copy.start()
        copies.append(copy)
    for copy in copies:
        copy.wait()
    sums_ref[...] = total[...]


def split_three(value):
    high = value.astype(jnp.bfloat16)
    rest = value - high.astype(jnp.float32)
    middle = rest.astype(jnp.bfloat16)
    low = (rest - middle.astype(jnp.float32)).astype(jnp.bfloat16)
    return high, middle, low


def inverse_factor(gram):
    size = gram.shape[0]
    count = size // 8
    tiles = [gram[8 * t : 8 * t + 8, :] for t in range(count)]
    lane = lax.broadcasted_iota(jnp.int32, (8, size), 1)
    sub = lax.broadcasted_iota(jnp.int32, (8, size), 0)

    def spread_row(tile, k):
        return jnp.broadcast_to(tile[k : k + 1, :], (8, size))

    def spread_columns(tile, panel):
        return [
            jnp.broadcast_to(tile[:, 8 * panel + k : 8 * panel + k + 1], (8, size))
            for k in range(8)
        ]

    for panel in range(count):
        tile = tiles[panel]
        columns = spread_columns(tile, panel)
        later_rows = []
        factors = []
        for k in range(8):
            here = lane == 8 * panel + k
            reciprocal = 1.0 / spread_row(columns[k], k)
            scaled = jnp.where(here, 1.0, spread_row(tile, k)) * reciprocal
            later_rows.append(
                jnp.where((lane > 8 * panel + k) & (lane < 8 * panel + 8), 0.0, scaled)
            )
            factors.append({m: spread_row(columns[m], k) * reciprocal for m in range(k + 1, 8)})
            below = sub > k
            lead = jnp.where(below, columns[k], 0.0)
            tile = jnp.where(here & below, 0.0, tile) - lead * scaled
            for m in range(k + 1, 8):
                columns[m] = columns[m] - lead * factors[k][m]
        tiles[panel] = tile
        for t in range(panel + 1, count):
            tile = tiles[t]
            columns = spread_columns(tile, panel)
            tile = jnp.where((lane >= 8 * panel) & (lane < 8 * panel + 8), 0.0, tile)
            for k in range(8):
                tile = tile - columns[k] * later_rows[k]
                for m in range(k + 1, 8):
                    columns[m] = columns[m] - columns[k] * factors[k][m]
            tiles[t] = tile
    inverse = []
    for t in range(size // 8):
        diagonal = lane == sub + 8 * t
        pivots = jnp.sum(jnp.where(diagonal, tiles[t], 0.0), axis=1, keepdims=True)
        unit = jnp.where(diagonal, 1.0, jnp.where(lane < sub + 8 * t, tiles[t], 0.0))
        inverse.append(unit / jnp.sqrt(pivots))
    return jnp.concatenate(inverse, axis=0)


def basis_kernel(total_rows, sums_ref, trial_ref, sigma_ref, projected_ref, basis_ref):
    size = sums_ref.shape[1]
    scale = 1.0 / total_rows
    overlap = sums_ref[0:size, :] * scale
    projected = sums_ref[size : 2 * size, :] * scale
    projected_ref[...] = projected
    square = sums_ref[2 * size : 3 * size, :] * scale
    row = lax.broadcasted_iota(jnp.int32, (size, size), 0)
    lane = lax.broadcasted_iota(jnp.int32, (size, size), 1)
    middle = jnp.where(row == lane, 2.0, 0.0) - overlap
    folded = jnp.dot(middle, projected, precision=HIGHEST, preferred_element_type=jnp.float32)
    gram = square - lax.dot_general(
        projected, folded, (((0,), (0,)), ((), ())),
        precision=HIGHEST, preferred_element_type=jnp.float32,
    )
    inverse = inverse_factor(gram)
    upper = inverse.T
    pulled = jnp.dot(projected, upper, precision=HIGHEST, preferred_element_type=jnp.float32)
    weights = jnp.concatenate([upper, 0.0 - pulled], axis=0)
    both = jnp.concatenate([sigma_ref[...], trial_ref[...]], axis=1)
    result = None
    for term in reversed(split_three(weights)):
        product = jnp.dot(both, term, preferred_element_type=jnp.float32)
        result = product if result is None else result + product
    basis_ref[...] = result


def on_device(n_blk, n_col, trial, omega, table, block_type, cycle_offset, source_block):
    row_count, vec_count = trial.shape
    pair_block = table.shape[1]
    blocks = row_count // pair_block
    near = max(size for size in (4, 2, 1) if n_blk % size == 0)
    group = near * n_col
    far = n_blk // near
    rows = 3 * vec_count
    piece = rows // group
    vmem = pl.BlockSpec(memory_space=pltpu.VMEM)
    smem = pl.BlockSpec(memory_space=pltpu.SMEM)
    hbm = pl.BlockSpec(memory_space=pltpu.HBM)
    dma = pltpu.SemaphoreType.DMA
    sigma, sums = pl.pallas_call(
        functools.partial(couple_kernel, n_blk, n_col, near),
        out_shape=(
            jax.ShapeDtypeStruct((row_count, vec_count), jnp.bfloat16),
            jax.ShapeDtypeStruct((rows, vec_count), jnp.float32),
        ),
        in_specs=[smem, smem, smem, hbm, hbm, hbm],
        out_specs=(vmem, vmem),
        scratch_shapes=[
            pltpu.VMEM(table.shape, jnp.bfloat16),
            pltpu.VMEM((2 * REACH + 1, blocks, pair_block, vec_count), jnp.bfloat16),
            pltpu.VMEM((blocks, pair_block), jnp.float32),
            pltpu.VMEM((rows, vec_count), jnp.float32),
            pltpu.VMEM((group - 1, piece, vec_count), jnp.float32),
            pltpu.VMEM((far, piece, vec_count), jnp.float32),
            pltpu.VMEM((rows, vec_count), jnp.float32),
            dma((3,)),
            dma((8, PARTS)),
            dma((8, PARTS)),
            dma((group - 1,)),
            dma((group - 1,)),
            dma((far - 1,)),
            dma((far - 1,)),
            dma((group - 1,)),
            dma((group - 1,)),
        ],
        compiler_params=pltpu.CompilerParams(
            collective_id=0, has_side_effects=True, vmem_limit_bytes=60 << 20
        ),
        name="couple",
    )(
        block_type,
        cycle_offset,
        source_block,
        trial.reshape(blocks, pair_block, vec_count),
        omega.reshape(blocks, pair_block),
        table,
    )
    projected, basis = pl.pallas_call(
        functools.partial(basis_kernel, row_count * n_blk * n_col),
        out_shape=(
            jax.ShapeDtypeStruct((vec_count, vec_count), jnp.float32),
            jax.ShapeDtypeStruct((row_count, vec_count), jnp.float32),
        ),
        in_specs=[vmem] * 3,
        out_specs=(vmem, vmem),
        compiler_params=pltpu.CompilerParams(vmem_limit_bytes=60 << 20),
        name="basis",
    )(sums, trial, sigma)
    return (sigma, projected, basis)


def solution(mesh):
    placed = (
        P(("blk", "col"), None),
        P(("blk", "col")),
        P(),
        P(("blk", "col"), None),
        P(("blk", "col"), None),
        P(("blk", "col"), None),
    )
    return jax.shard_map(
        functools.partial(on_device, mesh.shape["blk"], mesh.shape["col"]),
        mesh=mesh,
        in_specs=placed,
        out_specs=(P(("blk", "col"), None), P(), P(("blk", "col"), None)),
        check_vma=False,
    )
```

```python
import functools

import jax
import jax.numpy as jnp
from jax import lax
from jax.experimental import pallas as pl
from jax.experimental.pallas import tpu as pltpu
from jax.sharding import PartitionSpec as P

REACH = 4
MESH = pl.DeviceIdType.MESH
HIGHEST = lax.Precision.HIGHEST
PARTS = 4


def wrap(index, count):
    return lax.rem(index + count, count)


def couple_kernel(
    n_blk, n_col, near,
    kinds_ref, cycle_ref, source_ref, trial_hbm, omega_hbm, table_hbm,
    sigma_ref, sums_ref,
    table_ref, slabs, across, omega_ref, part, gathered, ring, total,
    local_sems, g_send, g_recv, r_send, r_recv, z_send, z_recv, a_send, a_recv,
):
    blocks, pair_block, vec_count = trial_hbm.shape
    per_row = kinds_ref.shape[1]
    rows = part.shape[0]
    me_b = lax.axis_index("blk")
    me_c = lax.axis_index("col")
    group = near * n_col
    far = n_blk // near
    piece = rows // group
    low = lax.rem(me_b, near)
    high = me_b // near
    mine = low * n_col + me_c

    def near_id(index):
        return (high * near + index // n_col, lax.rem(index, n_col))

    def far_id(index):
        return (index * near + low, me_c)

    keep_own = pltpu.make_async_copy(trial_hbm, slabs.at[REACH], local_sems.at[0])
    keep_own.start()
    load_omega = pltpu.make_async_copy(omega_hbm, omega_ref, local_sems.at[1])
    load_omega.start()
    load_table = pltpu.make_async_copy(table_hbm, table_ref, local_sems.at[2])
    load_table.start()

    barrier = pltpu.get_barrier_semaphore()
    for step in range(1, far):
        pl.semaphore_signal(
            barrier, inc=1, device_id=far_id(wrap(high + step, far)), device_id_type=MESH
        )
    for step in range(1, group):
        pl.semaphore_signal(
            barrier, inc=1, device_id=near_id(wrap(mine + step, group)), device_id_type=MESH
        )
    pl.semaphore_wait(barrier, group - 1 + far - 1)

    x = lax.rem(low, 2)
    y = low // 2
    up = wrap(me_b + REACH, n_blk)
    down = wrap(me_b - REACH, n_blk)
    side_x = me_b + 1 - 2 * x
    side_y = me_b + 2 - 4 * y
    span = blocks // PARTS

    def message(number, h, source, slot, target):
        rows_of = pl.ds(h * span, span)
        return pltpu.make_async_remote_copy(
            src_ref=trial_hbm.at[rows_of] if source is None else slabs.at[source, rows_of],
            dst_ref=slabs.at[slot, rows_of],
            send_sem=g_send.at[number, h],
            recv_sem=g_recv.at[number, h],
            device_id=(target, me_c),
            device_id_type=MESH,
        )

    halves = range(PARTS)
    to_up = [message(0, h, None, 0, up) for h in halves]
    to_down = [message(1, h, None, 2 * REACH, down) for h in halves]
    own_x = [message(2, h, None, 3 + 2 * x, side_x) for h in halves]
    own_y = [message(3, h, None, 2 + 4 * y, side_y) for h in halves]
    pass_y = [message(4, h, 5 - 2 * x, 3 - 2 * x + 4 * y, side_y) for h in halves]
    far_x = [message(5, h, 8 - 8 * x, 7 - 6 * x, side_x) for h in halves]
    far_y = [message(6, h, 8 - 8 * y, 6 - 4 * y, side_y) for h in halves]
    pass_x = [message(7, h, 2 + 4 * y, 1 + 4 * y + 2 * x, side_x) for h in halves]

    def far_arrival(bit, h):
        return pltpu.make_async_remote_copy(
            src_ref=trial_hbm.at[pl.ds(h * span, span)],
            dst_ref=slabs.at[8 - 8 * bit, pl.ds(h * span, span)],
            send_sem=g_send.at[1 - bit, h],
            recv_sem=g_recv.at[1 - bit, h],
            device_id=(up, me_c),
            device_id_type=MESH,
        )

    for h in halves:
        to_up[h].start()
        to_down[h].start()
        own_x[h].start()
        own_y[h].start()

    keep_own.wait()
    own = slabs[REACH].reshape(blocks * pair_block, vec_count)
    across[...] = own.T
    part[0:vec_count, :] = jnp.dot(across[...], own, preferred_element_type=jnp.float32)

    for h in halves:
        own_x[h].wait_recv()
        pass_y[h].start()
    for h in halves:
        far_arrival(x, h).wait_recv()
        far_x[h].start()

        @pl.when(x == y)
        def _():
            far_y[h].start()

    for h in halves:
        far_arrival(1 - x, h).wait_recv()

        @pl.when(x != y)
        def _():
            far_y[h].start()

    for h in halves:
        far_y[h].wait_recv()
        pass_x[h].start()
    load_omega.wait()
    load_table.wait()
    for h in halves:
        own_y[h].wait_recv()
        pass_y[h].wait_recv()
        far_x[h].wait_recv()
        pass_x[h].wait_recv()
    for sent in (to_up, to_down, own_x, own_y, pass_y, far_x, far_y, pass_x):
        for h in halves:
            sent[h].wait_send()

    chunk = max(size for size in range(1, 9) if per_row % size == 0)
    row_id = lax.broadcasted_iota(jnp.int32, (pair_block, pair_block), 0)
    lane_id = lax.broadcasted_iota(jnp.int32, (pair_block, pair_block), 1)

    def one_block(r, carry):
        energy = jnp.broadcast_to(omega_ref[pl.ds(r, 1), :], (pair_block, pair_block))
        column = jnp.sum(jnp.where(row_id == lane_id, energy, 0.0), axis=1, keepdims=True)
        acc = column * slabs[REACH, r].astype(jnp.float32)
        for start in range(0, per_row, chunk):
            coeffs = []
            sources = []
            for j in range(start, start + chunk):
                coeffs.append(table_ref[kinds_ref[r, j]])
                sources.append(slabs[cycle_ref[r, j] + REACH, source_ref[r, j]])
            acc = acc + jnp.dot(
                jnp.concatenate(coeffs, axis=1),
                jnp.concatenate(sources, axis=0),
                preferred_element_type=jnp.float32,
            )
        sigma_ref[pl.ds(pl.multiple_of(r * pair_block, pair_block), pair_block), :] = acc.astype(
            jnp.bfloat16
        )
        return carry

    lax.fori_loop(0, blocks, one_block, 0)

    sigma = sigma_ref[...]
    both = jnp.concatenate([across[...], sigma.T], axis=0)
    part[vec_count : 3 * vec_count, :] = jnp.dot(
        both, sigma, preferred_element_type=jnp.float32
    )

    copies = []
    for step in range(1, group):
        peer = wrap(mine + step, group)
        copy = pltpu.make_async_remote_copy(
            src_ref=part.at[pl.ds(pl.multiple_of(peer * piece, 8), piece)],
            dst_ref=gathered.at[step - 1],
            send_sem=r_send.at[step - 1],
            recv_sem=r_recv.at[step - 1],
            device_id=near_id(peer),
            device_id_type=MESH,
        )
        copy.start()
        copies.append(copy)
    piece_sum = part[pl.ds(pl.multiple_of(mine * piece, 8), piece), :]
    for step, copy in enumerate(copies):
        copy.wait()
        piece_sum = piece_sum + gathered[step]
    ring[high] = piece_sum

    copies = []
    for step in range(1, far):
        copy = pltpu.make_async_remote_copy(
            src_ref=ring.at[high],
            dst_ref=ring.at[high],
            send_sem=z_send.at[step - 1],
            recv_sem=z_recv.at[step - 1],
            device_id=far_id(wrap(high + step, far)),
            device_id_type=MESH,
        )
        copy.start()
        copies.append(copy)
    for copy in copies:
        copy.wait()
    piece_sum = ring[0]
    for index in range(1, far):
        piece_sum = piece_sum + ring[index]
    my_rows = pl.ds(pl.multiple_of(mine * piece, 8), piece)
    total[my_rows, :] = piece_sum

    copies = []
    for step in range(1, group):
        copy = pltpu.make_async_remote_copy(
            src_ref=total.at[my_rows],
            dst_ref=total.at[my_rows],
            send_sem=a_send.at[step - 1],
            recv_sem=a_recv.at[step - 1],
            device_id=near_id(wrap(mine + step, group)),
            device_id_type=MESH,
        )
        copy.start()
        copies.append(copy)
    for copy in copies:
        copy.wait()
    sums_ref[...] = total[...]


def split_three(value):
    high = value.astype(jnp.bfloat16)
    rest = value - high.astype(jnp.float32)
    middle = rest.astype(jnp.bfloat16)
    low = (rest - middle.astype(jnp.float32)).astype(jnp.bfloat16)
    return high, middle, low


def inverse_factor(gram):
    size = gram.shape[0]
    count = size // 8
    tiles = [gram[8 * t : 8 * t + 8, :] for t in range(count)]
    lane = lax.broadcasted_iota(jnp.int32, (8, size), 1)
    sub = lax.broadcasted_iota(jnp.int32, (8, size), 0)

    def spread_row(tile, k):
        return jnp.broadcast_to(tile[k : k + 1, :], (8, size))

    def spread_columns(tile, panel):
        return [
            jnp.broadcast_to(tile[:, 8 * panel + k : 8 * panel + k + 1], (8, size))
            for k in range(8)
        ]

    for panel in range(count):
        tile = tiles[panel]
        columns = spread_columns(tile, panel)
        later_rows = []
        factors = []
        for k in range(8):
            here = lane == 8 * panel + k
            reciprocal = 1.0 / spread_row(columns[k], k)
            scaled = jnp.where(here, 1.0, spread_row(tile, k)) * reciprocal
            later_rows.append(
                jnp.where((lane > 8 * panel + k) & (lane < 8 * panel + 8), 0.0, scaled)
            )
            factors.append({m: spread_row(columns[m], k) * reciprocal for m in range(k + 1, 8)})
            below = sub > k
            lead = jnp.where(below, columns[k], 0.0)
            tile = jnp.where(here & below, 0.0, tile) - lead * scaled
            for m in range(k + 1, 8):
                columns[m] = columns[m] - lead * factors[k][m]
        tiles[panel] = tile
        for t in range(panel + 1, count):
            tile = tiles[t]
            columns = spread_columns(tile, panel)
            tile = jnp.where((lane >= 8 * panel) & (lane < 8 * panel + 8), 0.0, tile)
            for k in range(8):
                tile = tile - columns[k] * later_rows[k]
                for m in range(k + 1, 8):
                    columns[m] = columns[m] - columns[k] * factors[k][m]
            tiles[t] = tile
    inverse = []
    for t in range(size // 8):
        diagonal = lane == sub + 8 * t
        pivots = jnp.sum(jnp.where(diagonal, tiles[t], 0.0), axis=1, keepdims=True)
        unit = jnp.where(diagonal, 1.0, jnp.where(lane < sub + 8 * t, tiles[t], 0.0))
        inverse.append(unit / jnp.sqrt(pivots))
    return jnp.concatenate(inverse, axis=0)


def basis_kernel(
    total_rows, sums_ref, trial_ref, coupled_ref, sigma_ref, projected_ref, basis_ref
):
    size = sums_ref.shape[1]
    scale = 1.0 / total_rows
    overlap = sums_ref[0:size, :] * scale
    projected = sums_ref[size : 2 * size, :] * scale
    projected_ref[...] = projected
    square = sums_ref[2 * size : 3 * size, :] * scale
    row = lax.broadcasted_iota(jnp.int32, (size, size), 0)
    lane = lax.broadcasted_iota(jnp.int32, (size, size), 1)
    middle = jnp.where(row == lane, 2.0, 0.0) - overlap
    folded = jnp.dot(middle, projected, precision=HIGHEST, preferred_element_type=jnp.float32)
    gram = square - lax.dot_general(
        projected, folded, (((0,), (0,)), ((), ())),
        precision=HIGHEST, preferred_element_type=jnp.float32,
    )
    inverse = inverse_factor(gram)
    upper = inverse.T
    pulled = jnp.dot(projected, upper, precision=HIGHEST, preferred_element_type=jnp.float32)
    weights = jnp.concatenate([upper, 0.0 - pulled], axis=0)
    coupled = coupled_ref[...]
    sigma_ref[...] = coupled
    both = jnp.concatenate([coupled, trial_ref[...]], axis=1)
    result = None
    for term in reversed(split_three(weights)):
        product = jnp.dot(both, term, preferred_element_type=jnp.float32)
        result = product if result is None else result + product
    basis_ref[...] = result


def on_device(n_blk, n_col, trial, omega, table, block_type, cycle_offset, source_block):
    row_count, vec_count = trial.shape
    pair_block = table.shape[1]
    blocks = row_count // pair_block
    near = max(size for size in (4, 2, 1) if n_blk % size == 0)
    group = near * n_col
    far = n_blk // near
    rows = 3 * vec_count
    piece = rows // group
    vmem = pl.BlockSpec(memory_space=pltpu.VMEM)
    smem = pl.BlockSpec(memory_space=pltpu.SMEM)
    hbm = pl.BlockSpec(memory_space=pltpu.HBM)
    dma = pltpu.SemaphoreType.DMA
    coupled, sums = pl.pallas_call(
        functools.partial(couple_kernel, n_blk, n_col, near),
        out_shape=(
            jax.ShapeDtypeStruct((row_count, vec_count), jnp.bfloat16),
            jax.ShapeDtypeStruct((rows, vec_count), jnp.float32),
        ),
        in_specs=[smem, smem, smem, hbm, hbm, hbm],
        out_specs=(vmem, vmem),
        scratch_shapes=[
            pltpu.VMEM(table.shape, jnp.bfloat16),
            pltpu.VMEM((2 * REACH + 1, blocks, pair_block, vec_count), jnp.bfloat16),
            pltpu.VMEM((vec_count, row_count), jnp.bfloat16),
            pltpu.VMEM((blocks, pair_block), jnp.float32),
            pltpu.VMEM((rows, vec_count), jnp.float32),
            pltpu.VMEM((group - 1, piece, vec_count), jnp.float32),
            pltpu.VMEM((far, piece, vec_count), jnp.float32),
            pltpu.VMEM((rows, vec_count), jnp.float32),
            dma((3,)),
            dma((8, PARTS)),
            dma((8, PARTS)),
            dma((group - 1,)),
            dma((group - 1,)),
            dma((far - 1,)),
            dma((far - 1,)),
            dma((group - 1,)),
            dma((group - 1,)),
        ],
        compiler_params=pltpu.CompilerParams(
            collective_id=0, has_side_effects=True, vmem_limit_bytes=60 << 20
        ),
        name="couple",
    )(
        block_type,
        cycle_offset,
        source_block,
        trial.reshape(blocks, pair_block, vec_count),
        omega.reshape(blocks, pair_block),
        table,
    )
    sigma, projected, basis = pl.pallas_call(
        functools.partial(basis_kernel, row_count * n_blk * n_col),
        out_shape=(
            jax.ShapeDtypeStruct((row_count, vec_count), jnp.bfloat16),
            jax.ShapeDtypeStruct((vec_count, vec_count), jnp.float32),
            jax.ShapeDtypeStruct((row_count, vec_count), jnp.float32),
        ),
        in_specs=[vmem] * 3,
        out_specs=(vmem, vmem, vmem),
        compiler_params=pltpu.CompilerParams(vmem_limit_bytes=60 << 20),
        name="basis",
    )(sums, trial, coupled)
    return (sigma, projected, basis)


def solution(mesh):
    placed = (
        P(("blk", "col"), None),
        P(("blk", "col")),
        P(),
        P(("blk", "col"), None),
        P(("blk", "col"), None),
        P(("blk", "col"), None),
    )
    return jax.shard_map(
        functools.partial(on_device, mesh.shape["blk"], mesh.shape["col"]),
        mesh=mesh,
        in_specs=placed,
        out_specs=(P(("blk", "col"), None), P(), P(("blk", "col"), None)),
        check_vma=False,
    )
```

```python
import functools

import jax
import jax.numpy as jnp
from jax import lax
from jax.experimental import pallas as pl
from jax.experimental.pallas import tpu as pltpu
from jax.sharding import PartitionSpec as P

REACH = 4
MESH = pl.DeviceIdType.MESH
HIGHEST = lax.Precision.HIGHEST
PARTS = 4


def wrap(index, count):
    return lax.rem(index + count, count)


def couple_kernel(
    n_blk, n_col, near,
    kinds_ref, cycle_ref, source_ref, trial_hbm, omega_hbm, table_hbm,
    sigma_ref, sums_ref,
    table_ref, slabs, across, omega_ref, part, gathered, ring, total,
    local_sems, g_send, g_recv, r_send, r_recv, z_send, z_recv, a_send, a_recv,
):
    blocks, pair_block, vec_count = trial_hbm.shape
    per_row = kinds_ref.shape[1]
    rows = part.shape[0]
    me_b = lax.axis_index("blk")
    me_c = lax.axis_index("col")
    group = near * n_col
    far = n_blk // near
    piece = rows // group
    low = lax.rem(me_b, near)
    high = me_b // near
    mine = low * n_col + me_c

    def near_id(index):
        return (high * near + index // n_col, lax.rem(index, n_col))

    def far_id(index):
        return (index * near + low, me_c)

    keep_own = pltpu.make_async_copy(trial_hbm, slabs.at[REACH], local_sems.at[0])
    keep_own.start()
    load_omega = pltpu.make_async_copy(omega_hbm, omega_ref, local_sems.at[1])
    load_omega.start()
    load_table = pltpu.make_async_copy(table_hbm, table_ref, local_sems.at[2])
    load_table.start()

    barrier = pltpu.get_barrier_semaphore()
    for step in range(1, far):
        pl.semaphore_signal(
            barrier, inc=1, device_id=far_id(wrap(high + step, far)), device_id_type=MESH
        )
    for step in range(1, group):
        pl.semaphore_signal(
            barrier, inc=1, device_id=near_id(wrap(mine + step, group)), device_id_type=MESH
        )
    pl.semaphore_wait(barrier, group - 1 + far - 1)

    x = lax.rem(low, 2)
    y = low // 2
    up = wrap(me_b + REACH, n_blk)
    down = wrap(me_b - REACH, n_blk)
    side_x = me_b + 1 - 2 * x
    side_y = me_b + 2 - 4 * y
    span = blocks // PARTS

    def message(number, h, source, slot, target):
        rows_of = pl.ds(h * span, span)
        return pltpu.make_async_remote_copy(
            src_ref=trial_hbm.at[rows_of] if source is None else slabs.at[source, rows_of],
            dst_ref=slabs.at[slot, rows_of],
            send_sem=g_send.at[number, h],
            recv_sem=g_recv.at[number, h],
            device_id=(target, me_c),
            device_id_type=MESH,
        )

    halves = range(PARTS)
    to_up = [message(0, h, None, 0, up) for h in halves]
    to_down = [message(1, h, None, 2 * REACH, down) for h in halves]
    own_x = [message(2, h, None, 3 + 2 * x, side_x) for h in halves]
    own_y = [message(3, h, None, 2 + 4 * y, side_y) for h in halves]
    pass_y = [message(4, h, 5 - 2 * x, 3 - 2 * x + 4 * y, side_y) for h in halves]
    far_x = [message(5, h, 8 - 8 * x, 7 - 6 * x, side_x) for h in halves]
    far_y = [message(6, h, 8 - 8 * y, 6 - 4 * y, side_y) for h in halves]
    pass_x = [message(7, h, 2 + 4 * y, 1 + 4 * y + 2 * x, side_x) for h in halves]

    def far_arrival(bit, h):
        return pltpu.make_async_remote_copy(
            src_ref=trial_hbm.at[pl.ds(h * span, span)],
            dst_ref=slabs.at[8 - 8 * bit, pl.ds(h * span, span)],
            send_sem=g_send.at[1 - bit, h],
            recv_sem=g_recv.at[1 - bit, h],
            device_id=(up, me_c),
            device_id_type=MESH,
        )

    for h in halves:

        @pl.when(high != far - 1)
        def _():
            to_up[h].start()

        @pl.when(high != 0)
        def _():
            to_down[h].start()

        own_x[h].start()
        own_y[h].start()

    keep_own.wait()
    own = slabs[REACH].reshape(blocks * pair_block, vec_count)
    across[...] = own.T
    part[0:vec_count, :] = jnp.dot(across[...], own, preferred_element_type=jnp.float32)

    for h in halves:
        own_x[h].wait_recv()
        pass_y[h].start()

        @pl.when(high == far - 1)
        def _():
            to_up[h].start()

        @pl.when(high == 0)
        def _():
            to_down[h].start()

    for h in halves:
        far_arrival(x, h).wait_recv()
        far_x[h].start()

        @pl.when(x == y)
        def _():
            far_y[h].start()

    for h in halves:
        far_arrival(1 - x, h).wait_recv()

        @pl.when(x != y)
        def _():
            far_y[h].start()

    for h in halves:
        far_y[h].wait_recv()
        pass_x[h].start()
    load_omega.wait()
    load_table.wait()
    for h in halves:
        own_y[h].wait_recv()
        pass_y[h].wait_recv()
        far_x[h].wait_recv()
        pass_x[h].wait_recv()

    chunk = max(size for size in range(1, 9) if per_row % size == 0)
    row_id = lax.broadcasted_iota(jnp.int32, (pair_block, pair_block), 0)
    lane_id = lax.broadcasted_iota(jnp.int32, (pair_block, pair_block), 1)

    def one_block(r, carry):
        energy = jnp.broadcast_to(omega_ref[pl.ds(r, 1), :], (pair_block, pair_block))
        column = jnp.sum(jnp.where(row_id == lane_id, energy, 0.0), axis=1, keepdims=True)
        acc = column * slabs[REACH, r].astype(jnp.float32)
        for start in range(0, per_row, chunk):
            coeffs = []
            sources = []
            for j in range(start, start + chunk):
                coeffs.append(table_ref[kinds_ref[r, j]])
                sources.append(slabs[cycle_ref[r, j] + REACH, source_ref[r, j]])
            acc = acc + jnp.dot(
                jnp.concatenate(coeffs, axis=1),
                jnp.concatenate(sources, axis=0),
                preferred_element_type=jnp.float32,
            )
        sigma_ref[pl.ds(pl.multiple_of(r * pair_block, pair_block), pair_block), :] = acc.astype(
            jnp.bfloat16
        )
        return carry

    lax.fori_loop(0, blocks, one_block, 0)
    for sent in (to_up, to_down, own_x, own_y, pass_y, far_x, far_y, pass_x):
        for h in halves:
            sent[h].wait_send()

    sigma = sigma_ref[...]
    both = jnp.concatenate([across[...], sigma.T], axis=0)
    part[vec_count : 3 * vec_count, :] = jnp.dot(
        both, sigma, preferred_element_type=jnp.float32
    )

    copies = []
    for step in range(1, group):
        peer = wrap(mine + step, group)
        copy = pltpu.make_async_remote_copy(
            src_ref=part.at[pl.ds(pl.multiple_of(peer * piece, 8), piece)],
            dst_ref=gathered.at[step - 1],
            send_sem=r_send.at[step - 1],
            recv_sem=r_recv.at[step - 1],
            device_id=near_id(peer),
            device_id_type=MESH,
        )
        copy.start()
        copies.append(copy)
    piece_sum = part[pl.ds(pl.multiple_of(mine * piece, 8), piece), :]
    for step, copy in enumerate(copies):
        copy.wait()
        piece_sum = piece_sum + gathered[step]
    ring[high] = piece_sum

    copies = []
    for step in range(1, far):
        copy = pltpu.make_async_remote_copy(
            src_ref=ring.at[high],
            dst_ref=ring.at[high],
            send_sem=z_send.at[step - 1],
            recv_sem=z_recv.at[step - 1],
            device_id=far_id(wrap(high + step, far)),
            device_id_type=MESH,
        )
        copy.start()
        copies.append(copy)
    for copy in copies:
        copy.wait()
    piece_sum = ring[0]
    for index in range(1, far):
        piece_sum = piece_sum + ring[index]
    my_rows = pl.ds(pl.multiple_of(mine * piece, 8), piece)
    total[my_rows, :] = piece_sum

    copies = []
    for step in range(1, group):
        copy = pltpu.make_async_remote_copy(
            src_ref=total.at[my_rows],
            dst_ref=total.at[my_rows],
            send_sem=a_send.at[step - 1],
            recv_sem=a_recv.at[step - 1],
            device_id=near_id(wrap(mine + step, group)),
            device_id_type=MESH,
        )
        copy.start()
        copies.append(copy)
    for copy in copies:
        copy.wait()
    sums_ref[...] = total[...]


def split_three(value):
    high = value.astype(jnp.bfloat16)
    rest = value - high.astype(jnp.float32)
    middle = rest.astype(jnp.bfloat16)
    low = (rest - middle.astype(jnp.float32)).astype(jnp.bfloat16)
    return high, middle, low


def inverse_factor(gram):
    size = gram.shape[0]
    count = size // 8
    tiles = [gram[8 * t : 8 * t + 8, :] for t in range(count)]
    lane = lax.broadcasted_iota(jnp.int32, (8, size), 1)
    sub = lax.broadcasted_iota(jnp.int32, (8, size), 0)

    def spread_row(tile, k):
        return jnp.broadcast_to(tile[k : k + 1, :], (8, size))

    def spread_columns(tile, panel):
        return [
            jnp.broadcast_to(tile[:, 8 * panel + k : 8 * panel + k + 1], (8, size))
            for k in range(8)
        ]

    for panel in range(count):
        tile = tiles[panel]
        columns = spread_columns(tile, panel)
        later_rows = []
        factors = []
        for k in range(8):
            here = lane == 8 * panel + k
            reciprocal = 1.0 / spread_row(columns[k], k)
            scaled = jnp.where(here, 1.0, spread_row(tile, k)) * reciprocal
            later_rows.append(
                jnp.where((lane > 8 * panel + k) & (lane < 8 * panel + 8), 0.0, scaled)
            )
            factors.append({m: spread_row(columns[m], k) * reciprocal for m in range(k + 1, 8)})
            below = sub > k
            lead = jnp.where(below, columns[k], 0.0)
            tile = jnp.where(here & below, 0.0, tile) - lead * scaled
            for m in range(k + 1, 8):
                columns[m] = columns[m] - lead * factors[k][m]
        tiles[panel] = tile
        for t in range(panel + 1, count):
            tile = tiles[t]
            columns = spread_columns(tile, panel)
            tile = jnp.where((lane >= 8 * panel) & (lane < 8 * panel + 8), 0.0, tile)
            for k in range(8):
                tile = tile - columns[k] * later_rows[k]
                for m in range(k + 1, 8):
                    columns[m] = columns[m] - columns[k] * factors[k][m]
            tiles[t] = tile
    inverse = []
    for t in range(size // 8):
        diagonal = lane == sub + 8 * t
        pivots = jnp.sum(jnp.where(diagonal, tiles[t], 0.0), axis=1, keepdims=True)
        unit = jnp.where(diagonal, 1.0, jnp.where(lane < sub + 8 * t, tiles[t], 0.0))
        inverse.append(unit / jnp.sqrt(pivots))
    return jnp.concatenate(inverse, axis=0)


def basis_kernel(
    total_rows, sums_ref, trial_ref, coupled_ref, sigma_ref, projected_ref, basis_ref
):
    size = sums_ref.shape[1]
    scale = 1.0 / total_rows
    overlap = sums_ref[0:size, :] * scale
    projected = sums_ref[size : 2 * size, :] * scale
    projected_ref[...] = projected
    square = sums_ref[2 * size : 3 * size, :] * scale
    row = lax.broadcasted_iota(jnp.int32, (size, size), 0)
    lane = lax.broadcasted_iota(jnp.int32, (size, size), 1)
    middle = jnp.where(row == lane, 2.0, 0.0) - overlap
    folded = jnp.dot(middle, projected, precision=HIGHEST, preferred_element_type=jnp.float32)
    gram = square - lax.dot_general(
        projected, folded, (((0,), (0,)), ((), ())),
        precision=HIGHEST, preferred_element_type=jnp.float32,
    )
    inverse = inverse_factor(gram)
    upper = inverse.T
    pulled = jnp.dot(projected, upper, precision=HIGHEST, preferred_element_type=jnp.float32)
    weights = jnp.concatenate([upper, 0.0 - pulled], axis=0)
    coupled = coupled_ref[...]
    sigma_ref[...] = coupled
    both = jnp.concatenate([coupled, trial_ref[...]], axis=1)
    result = None
    for term in reversed(split_three(weights)):
        product = jnp.dot(both, term, preferred_element_type=jnp.float32)
        result = product if result is None else result + product
    basis_ref[...] = result


def on_device(n_blk, n_col, trial, omega, table, block_type, cycle_offset, source_block):
    row_count, vec_count = trial.shape
    pair_block = table.shape[1]
    blocks = row_count // pair_block
    near = max(size for size in (4, 2, 1) if n_blk % size == 0)
    group = near * n_col
    far = n_blk // near
    rows = 3 * vec_count
    piece = rows // group
    vmem = pl.BlockSpec(memory_space=pltpu.VMEM)
    smem = pl.BlockSpec(memory_space=pltpu.SMEM)
    hbm = pl.BlockSpec(memory_space=pltpu.HBM)
    dma = pltpu.SemaphoreType.DMA
    coupled, sums = pl.pallas_call(
        functools.partial(couple_kernel, n_blk, n_col, near),
        out_shape=(
            jax.ShapeDtypeStruct((row_count, vec_count), jnp.bfloat16),
            jax.ShapeDtypeStruct((rows, vec_count), jnp.float32),
        ),
        in_specs=[smem, smem, smem, hbm, hbm, hbm],
        out_specs=(vmem, vmem),
        scratch_shapes=[
            pltpu.VMEM(table.shape, jnp.bfloat16),
            pltpu.VMEM((2 * REACH + 1, blocks, pair_block, vec_count), jnp.bfloat16),
            pltpu.VMEM((vec_count, row_count), jnp.bfloat16),
            pltpu.VMEM((blocks, pair_block), jnp.float32),
            pltpu.VMEM((rows, vec_count), jnp.float32),
            pltpu.VMEM((group - 1, piece, vec_count), jnp.float32),
            pltpu.VMEM((far, piece, vec_count), jnp.float32),
            pltpu.VMEM((rows, vec_count), jnp.float32),
            dma((3,)),
            dma((8, PARTS)),
            dma((8, PARTS)),
            dma((group - 1,)),
            dma((group - 1,)),
            dma((far - 1,)),
            dma((far - 1,)),
            dma((group - 1,)),
            dma((group - 1,)),
        ],
        compiler_params=pltpu.CompilerParams(
            collective_id=0, has_side_effects=True, vmem_limit_bytes=60 << 20
        ),
        name="couple",
    )(
        block_type,
        cycle_offset,
        source_block,
        trial.reshape(blocks, pair_block, vec_count),
        omega.reshape(blocks, pair_block),
        table,
    )
    sigma, projected, basis = pl.pallas_call(
        functools.partial(basis_kernel, row_count * n_blk * n_col),
        out_shape=(
            jax.ShapeDtypeStruct((row_count, vec_count), jnp.bfloat16),
            jax.ShapeDtypeStruct((vec_count, vec_count), jnp.float32),
            jax.ShapeDtypeStruct((row_count, vec_count), jnp.float32),
        ),
        in_specs=[vmem] * 3,
        out_specs=(vmem, vmem, vmem),
        compiler_params=pltpu.CompilerParams(vmem_limit_bytes=60 << 20),
        name="basis",
    )(sums, trial, coupled)
    return (sigma, projected, basis)


def solution(mesh):
    placed = (
        P(("blk", "col"), None),
        P(("blk", "col")),
        P(),
        P(("blk", "col"), None),
        P(("blk", "col"), None),
        P(("blk", "col"), None),
    )
    return jax.shard_map(
        functools.partial(on_device, mesh.shape["blk"], mesh.shape["col"]),
        mesh=mesh,
        in_specs=placed,
        out_specs=(P(("blk", "col"), None), P(), P(("blk", "col"), None)),
        check_vma=False,
    )
```
